32 devices in a mesh: dp: 2 (over x), ha: 4 (over z), wa: 4 (over y, core).
Axes of the slice: x: 2, y: 2, z: 4, core: 2. Of those that a mesh axis runs over, the one named last changes fastest.
Arguments:
- query_in: bfloat16 [2, 4, 4, 384, 512], P('dp', 'ha', 'wa'), may hold values from -30 to 30
- key_in: bfloat16 [2, 4, 4, 384, 512], P('dp', 'ha', 'wa'), may hold values from -6 to 6
- value_in: bfloat16 [2, 4, 4, 384, 512], P('dp', 'ha', 'wa'), may hold values from -6 to 6
- grad_out: bfloat16 [2, 4, 4, 384, 3072], P('dp', 'ha', 'wa'), may hold values from -1.5 to 1.5
- out_weight: bfloat16 [512, 3072], P('dp'), may hold values from -0.25 to 0.25
Outputs:
- outcome: bfloat16 [2, 4, 4, 384, 3072], P('dp', 'ha', 'wa')
- query_grad: float32 [2, 4, 4, 384, 512], P('dp', 'ha', 'wa')
- key_grad: float32 [2, 4, 4, 384, 512], P('dp', 'ha', 'wa')
- value_grad: float32 [2, 4, 4, 384, 512], P('dp', 'ha', 'wa')
- weight_grad: float32 [512, 3072], P('dp')
The draws below stay inside these ranges and needn't reach their ends.
All inputs are finite; a program needn't handle non-finite values.
Results may differ from the reference program's by a relative error of at most 0.035.
Values may be sent and summed in bfloat16 or wider, within the bound.
No kernel may reach another device: no remote copies, remote signals or barrier semaphores. Data moves between devices by JAX's collectives and lax.ppermute only.
A program may use at most 192 MiB of HBM per device.

```python
import jax
import jax.numpy as jnp
from jax import lax

D = 3072
HEADS = 4
F = 512
TILE = 384
CLIPS = 2
HTILES = 4
WTILES = 4


def key_field(key):
    base_key = jax.random.fold_in(key, 11)
    field_shape = (CLIPS, HTILES, WTILES, TILE, F)
    values_drawn = 1.5 * jax.random.truncated_normal(base_key, -4.0, 4.0, field_shape, jnp.float32)
    return values_drawn


def draw_key_in(key, part):
    return key_field(key).astype(jnp.bfloat16)


def draw_query_in(key, part):
    base_key = jax.random.fold_in(key, 12)
    field_shape = (CLIPS, HTILES, WTILES, TILE, F)
    values_drawn = 1.5 * jax.random.truncated_normal(base_key, -4.0, 4.0, field_shape, jnp.float32)
    return values_drawn.astype(jnp.bfloat16)


def levels(rng, dims, pieces, low, high):
    def one(position, parts):
        draws = jax.random.uniform(jax.random.fold_in(jax.random.fold_in(rng, 6), position), (parts,), jnp.float32, low / len(pieces), high / len(pieces))
        return jnp.repeat(jnp.exp(draws), dims[position] // parts).reshape((-1,) + (1,) * (len(dims) - position - 1))

    level = one(*pieces[0])
    for cut in pieces[1:]:
        level = level * one(*cut)
    return level


def normal_values(stream_key, shape, spread, most, split=(), kind=jnp.bfloat16):
    result = jax.random.normal(stream_key, shape, jnp.float32) * spread
    if len(split) > 0:
        result = levels(stream_key, shape, split, -0.22, 0.18) * result
    return jnp.clip(result, min=-most, max=most).astype(kind)


def setup_inputs(seed: int = 0) -> dict:
    splits = jax.random.split(jax.random.key(seed), 6)
    query_in = draw_query_in(jax.random.fold_in(splits[5], 71), 0)
    key_in = draw_key_in(jax.random.fold_in(splits[5], 71), 0)
    value_in = normal_values(splits[2], (CLIPS, HTILES, WTILES, TILE, F), 1.0, 6.0, ((0, 2), (1, 4), (2, 4)))
    grad_out = normal_values(splits[3], (CLIPS, HTILES, WTILES, TILE, D), 0.25, 1.5, ((0, 2), (1, 4), (2, 4)))
    out_weight = normal_values(splits[4], (F, D), F ** -0.5, 0.25, ((0, 2),))
    return dict(query_in=query_in, key_in=key_in, value_in=value_in, grad_out=grad_out, out_weight=out_weight)


SCALE_POWER = -0.5


def product(pattern, first_op, second_op):
    return jnp.einsum(pattern, first_op.astype(jnp.float32), second_op.astype(jnp.float32))


def stack_window(extended, tile_cols):
    window_parts = []
    for row_off in range(3):
        for col_off in range(3):
            window_parts.append(extended[row_off, col_off:col_off + tile_cols])
    stacked = jnp.stack(window_parts, axis=1)
    return stacked.reshape((tile_cols, 9 * stacked.shape[2]) + stacked.shape[3:])


def window_keep(row_ok, col_ok, tile_cols, tile_len):
    flag_list = []
    for row_off in range(3):
        for col_off in range(3):
            flag_list.append(jnp.logical_and(row_ok[row_off], col_ok[col_off:col_off + tile_cols]))
    stacked = jnp.stack(flag_list, axis=1)
    return jnp.repeat(stacked, tile_len, axis=1)


def spread_window(stacked, tile_cols, tile_len):
    window_parts = stacked.reshape((tile_cols, 3, 3, tile_len) + stacked.shape[2:])
    spread_rows = []
    for row_off in range(3):
        gathered = None
        for col_off in range(3):
            placed = jnp.pad(window_parts[:, row_off, col_off], ((col_off, 2 - col_off), (0, 0), (0, 0)))
            gathered = placed if gathered is None else gathered + placed
        spread_rows.append(gathered)
    return jnp.stack(spread_rows)


def attend_row(query_row, key_ext, value_ext, visible, head_count):
    tile_cols, tile_len, feature_width = query_row.shape
    head_dim = feature_width // head_count
    score_scale = head_dim ** SCALE_POWER
    query_heads = query_row.reshape(tile_cols, tile_len, head_count, head_dim)
    key_heads = stack_window(key_ext, tile_cols).reshape(tile_cols, 9 * tile_len, head_count, head_dim)
    value_heads = stack_window(value_ext, tile_cols).reshape(tile_cols, 9 * tile_len, head_count, head_dim)
    scores = product("jqhd,jkhd->jhqk", query_heads, key_heads) * score_scale
    scores = jnp.where(visible[:, None, None, :], scores, -1e30)
    row_max = jnp.max(scores, axis=-1, keepdims=True)
    log_norm = row_max + jnp.log(jnp.sum(jnp.exp(scores - row_max), axis=-1, keepdims=True))
    soft_probs = jnp.exp(scores - log_norm).astype(jnp.bfloat16)
    attended = product("jhqk,jkhd->jqhd", soft_probs, value_heads)
    attended = attended.reshape(tile_cols, tile_len, feature_width).astype(jnp.bfloat16)
    return attended, soft_probs, log_norm[..., 0]


def query_back(query_row, key_ext, value_ext, attended, grad_attn, soft_probs, head_count, with_keys):
    tile_cols, tile_len, feature_width = query_row.shape
    head_dim = feature_width // head_count
    score_scale = head_dim ** SCALE_POWER
    attended_heads = attended.astype(jnp.float32).reshape(tile_cols, tile_len, head_count, head_dim)
    grad_heads = grad_attn.reshape(tile_cols, tile_len, head_count, head_dim)
    row_delta = jnp.sum(attended_heads * grad_heads.astype(jnp.float32), axis=-1)
    row_delta = jnp.transpose(row_delta, (0, 2, 1))
    value_heads = stack_window(value_ext, tile_cols).reshape(tile_cols, 9 * tile_len, head_count, head_dim)
    prob_grad = product("jqhd,jkhd->jhqk", grad_heads, value_heads)
    score_grad = (soft_probs.astype(jnp.float32) * (prob_grad - row_delta[..., None])).astype(jnp.bfloat16)
    key_heads = stack_window(key_ext, tile_cols).reshape(tile_cols, 9 * tile_len, head_count, head_dim)
    query_grad = product("jhqk,jkhd->jqhd", score_grad, key_heads) * score_scale
    query_grad = query_grad.reshape(tile_cols, tile_len, feature_width)
    if not with_keys:
        return query_grad, row_delta
    query_heads = query_row.reshape(tile_cols, tile_len, head_count, head_dim)
    key_part = (product("jhqk,jqhd->jkhd", score_grad, query_heads) * score_scale).reshape(tile_cols, 9 * tile_len, feature_width)
    value_part = product("jhqk,jqhd->jkhd", soft_probs, grad_heads).reshape(tile_cols, 9 * tile_len, feature_width)
    return query_grad, row_delta, spread_window(key_part, tile_cols, tile_len), spread_window(value_part, tile_cols, tile_len)


def reference(query_in, key_in, value_in, grad_out, out_weight):
    clip_count, tile_rows, tile_cols, tile_len, feature_width = query_in.shape
    model_width = out_weight.shape[1]
    flat_grad = grad_out.reshape(-1, model_width)
    grad_attn = jnp.dot(flat_grad, out_weight.T, preferred_element_type=jnp.float32)
    grad_attn = grad_attn.astype(jnp.bfloat16).reshape(query_in.shape)
    pad_spec = ((1, 1), (1, 1), (0, 0), (0, 0))
    col_index = jnp.arange(tile_cols + 2, dtype=jnp.int32)
    col_ok = jnp.logical_and(col_index >= 1, col_index <= tile_cols)
    row_index_all = jnp.arange(tile_rows + 2, dtype=jnp.int32)
    row_flags = jnp.logical_and(row_index_all >= 1, row_index_all <= tile_rows)

    def one_clip(clip_data):
        queries, keys_clip, values_clip, grads_clip = clip_data
        key_pad = jnp.pad(keys_clip, pad_spec)
        value_pad = jnp.pad(values_clip, pad_spec)
        zero_pad = jnp.zeros(key_pad.shape, jnp.float32)

        def one_row(carried, row_index):
            key_grad_pad, value_grad_pad = carried
            key_ext = lax.dynamic_slice_in_dim(key_pad, row_index, 3, 0)
            value_ext = lax.dynamic_slice_in_dim(value_pad, row_index, 3, 0)
            row_ok = lax.dynamic_slice_in_dim(row_flags, row_index, 3, 0)
            visible = window_keep(row_ok, col_ok, tile_cols, tile_len)
            query_row = lax.dynamic_index_in_dim(queries, row_index, 0, keepdims=False)
            grad_row = lax.dynamic_index_in_dim(grads_clip, row_index, 0, keepdims=False)
            attended, soft_probs, log_norm = attend_row(query_row, key_ext, value_ext, visible, HEADS)
            query_grad, row_delta, key_part, value_part = query_back(query_row, key_ext, value_ext, attended, grad_row, soft_probs, HEADS, True)
            old_keys = lax.dynamic_slice_in_dim(key_grad_pad, row_index, 3, 0)
            key_grad_pad = lax.dynamic_update_slice_in_dim(key_grad_pad, old_keys + key_part, row_index, 0)
            old_values = lax.dynamic_slice_in_dim(value_grad_pad, row_index, 3, 0)
            value_grad_pad = lax.dynamic_update_slice_in_dim(value_grad_pad, old_values + value_part, row_index, 0)
            return (key_grad_pad, value_grad_pad), (attended, query_grad)

        final_pads, row_outputs = lax.scan(one_row, (zero_pad, zero_pad), jnp.arange(tile_rows, dtype=jnp.int32))
        return row_outputs[0], row_outputs[1], final_pads[0][1:-1, 1:-1], final_pads[1][1:-1, 1:-1]

    attended, query_grad, key_grad, value_grad = lax.map(one_clip, (query_in, key_in, value_in, grad_attn))
    flat_attn = attended.reshape(-1, feature_width)
    outcome = jnp.dot(flat_attn, out_weight, preferred_element_type=jnp.float32).astype(jnp.bfloat16)
    outcome = outcome.reshape(clip_count, tile_rows, tile_cols, tile_len, model_width)
    weight_grad = jnp.dot(flat_attn.T, flat_grad, preferred_element_type=jnp.float32)
    return (outcome, query_grad, key_grad, value_grad, weight_grad)
```

```python
import math

import jax
import jax.numpy as jnp
from jax import lax
from jax.experimental import pallas as pl
from jax.experimental.pallas import tpu as pltpu
from jax.sharding import PartitionSpec as P

HEADS = 4
BF = jnp.bfloat16
F32 = jnp.float32


def xor_send(value, axis, mask):
    count = lax.axis_size(axis)
    return lax.ppermute(value, axis, [(i, i ^ mask) for i in range(count)])


def step_send(value, axis, step):
    count = lax.axis_size(axis)
    pairs = [(i, i + step) for i in range(count) if 0 <= i + step < count]
    return lax.ppermute(value, axis, pairs)


def sds(shape, dtype):
    return jax.ShapeDtypeStruct(shape, dtype)


def full_spec(shape):
    zeros = (0,) * len(shape)
    return pl.BlockSpec(tuple(shape), lambda *_: zeros)


def call(kernel, scalars, args, outs, grid=(1,), in_specs=None, out_specs=None, scratch=(), flops=0, exps=0):
    in_specs = [full_spec(a.shape) if s is None else s for a, s in zip(args, in_specs or [None] * len(args))]
    out_specs = [full_spec(o.shape) if s is None else s for o, s in zip(outs, out_specs or [None] * len(outs))]
    moved = sum(a.size * a.dtype.itemsize for a in args) + sum(o.size * jnp.dtype(o.dtype).itemsize for o in outs)
    return pl.pallas_call(
        kernel,
        out_shape=list(outs),
        grid_spec=pltpu.PrefetchScalarGridSpec(
            num_scalar_prefetch=1,
            grid=grid,
            in_specs=in_specs,
            out_specs=out_specs,
            scratch_shapes=list(scratch),
        ),
        cost_estimate=pl.CostEstimate(flops=flops, transcendentals=exps, bytes_accessed=moved),
        compiler_params=pltpu.CompilerParams(
            dimension_semantics=("arbitrary",) * len(grid), vmem_limit_bytes=56 << 20
        ),
    )(scalars, *args)


def dot(a, b, dims):
    return lax.dot_general(a, b, (dims, ((), ())), preferred_element_type=F32)


NN = ((1,), (0,))
NT = ((1,), (1,))
TN = ((0,), (0,))


def lanes(index, width=128):
    return pl.ds(pl.multiple_of(index * width, width), width)


def pack_kernel(sc, q, k, v, *outs):
    w = sc[0]
    for m in range(4):
        cols = lanes(w ^ m)
        outs[m][0] = k[:, cols]
        outs[m][1] = v[:, cols]
        outs[4 + m][...] = q[:, cols]


def grad_attn_kernel(sc, g, w_own, w_a, w_b, *refs):
    outs, acc, by_head = refs[:4], refs[4], refs[5]
    step = pl.program_id(0)

    @pl.when(step == 0)
    def _():
        acc[...] = jnp.zeros_like(acc)

    part = g[...]
    acc[:, :256] += dot(part, w_own[...], NT)
    acc[:, 256:384] += dot(part, w_a[...], NT)
    acc[:, 384:] += dot(part, w_b[...], NT)

    @pl.when(step == pl.num_programs(0) - 1)
    def _():
        for slot in range(4):
            by_head[sc[1 + slot]] = acc[:, slot * 128 : slot * 128 + 128].astype(BF)
        for m in range(4):
            outs[m][...] = by_head[sc[0] ^ m]


def forward_kernel(factor, sc, *refs):
    q_in, kv_in = refs[:4], refs[4:16]
    att_m, (att_b, inv_b, p_b) = refs[16:20], refs[20:23]
    ks, vs, qs, ss, mx, acc = refs[23:]
    b = pl.program_id(0)
    w, row_lo, row_hi = sc[0], sc[1], sc[2]

    @pl.when(b == 0)
    def _():
        for m in range(4):
            col = w ^ m
            qs[col] = q_in[m][...]
            for r in range(3):
                ks[r, col] = kv_in[r * 4 + m][0]
                vs[r, col, :, :128] = kv_in[r * 4 + m][1]
                vs[r, col, :, 128:] = jnp.ones((vs.shape[2], 128), BF)

    q = qs[b]
    col_lo = jnp.maximum(b - 1, 0)
    col_hi = jnp.minimum(b + 2, 4)
    mx[...] = jnp.full(mx.shape, -jnp.inf, F32)

    def score_row(r, carry):
        def score_col(c, inner):
            s = dot(q, ks[r, c], NT)
            ss[r * 3 + c - b + 1] = s
            best = mx[...]
            for i in range(s.shape[1] // 128):
                best = jnp.maximum(best, s[:, i * 128 : i * 128 + 128])
            mx[...] = best
            return inner

        return lax.fori_loop(col_lo, col_hi, score_col, carry)

    lax.fori_loop(row_lo, row_hi, score_row, 0)
    top = jnp.max(mx[...], axis=1, keepdims=True)
    acc[...] = jnp.zeros_like(acc)

    def prob_row(r, carry):
        def prob_col(c, inner):
            p = jnp.exp2((ss[r * 3 + c - b + 1] - top) * factor).astype(BF)
            p_b[0, r, c - b + 1] = p
            acc[...] += dot(p, vs[r, c], NN)
            return inner

        return lax.fori_loop(col_lo, col_hi, prob_col, carry)

    lax.fori_loop(row_lo, row_hi, prob_row, 0)
    inverse = 1.0 / acc[:, 128:]
    out = (acc[:, :128] * inverse).astype(BF)
    att_b[0] = out
    inv_b[0] = inverse
    for m in range(4):

        @pl.when((b ^ w) == m)
        def _():
            att_m[m][...] = out


def backward_kernel(rows, scale, sc, *refs):
    n = len(rows)
    q_in, kv_in, do_in = refs[:4], refs[4 : 4 + 4 * n], refs[4 + 4 * n : 8 + 4 * n]
    att_b, inv_b = refs[8 + 4 * n : 10 + 4 * n]
    p_in = refs[10 + 4 * n : 10 + 5 * n]
    rest = refs[10 + 5 * n :]
    own = rows == (1,)
    if own:
        dq_prev, rest = rest[0], rest[1:]
        dq_m, dkv_out, rest = rest[:4], rest[4:5], rest[5:]
    else:
        dq_out, dkv_out, rest = rest[0], rest[1 : 1 + n], rest[1 + n :]
    ks, vs, qs, dos, dk, dv, dq = rest
    b = pl.program_id(0)
    w, row_lo, row_hi = sc[0], sc[1], sc[2]

    @pl.when(b == 0)
    def _():
        for m in range(4):
            col = w ^ m
            qs[col] = q_in[m][...]
            dos[col] = do_in[m][...]
            for i in range(n):
                ks[i, col] = kv_in[i * 4 + m][0]
                vs[i, col] = kv_in[i * 4 + m][1]
        dk[...] = jnp.zeros_like(dk)
        dv[...] = jnp.zeros_like(dv)

    q = qs[b]
    inverse = inv_b[0]
    grad = dos[b].astype(F32)
    delta = jnp.sum(att_b[0].astype(F32) * grad, axis=1, keepdims=True) * inverse[:, :1]
    grad = (grad * inverse).astype(BF)
    dq[...] = jnp.zeros_like(dq)
    col_lo = jnp.maximum(b - 1, 0)
    col_hi = jnp.minimum(b + 2, 4)
    for i, r in enumerate(rows):

        def one_row():
            def one_col(c, carry):
                p = p_in[i][0, 0, c - b + 1]
                dp = dot(grad, vs[i, c], NT)
                ds = (p.astype(F32) * (dp - delta)).astype(BF)
                dq[...] += dot(ds, ks[i, c], NN)
                dk[i, c] += dot(ds, q, TN)
                dv[i, c] += dot(p, grad, TN)
                return carry

            lax.fori_loop(col_lo, col_hi, one_col, 0)

        if own:
            one_row()
        else:
            pl.when((row_lo <= r) & (r < row_hi))(one_row)

    if own:
        total = (dq[...] + dq_prev[0]) * scale
        for m in range(4):

            @pl.when((b ^ w) == m)
            def _():
                dq_m[m][...] = total.astype(dq_m[m].dtype)
    else:
        dq_out[0] = dq[...]

    @pl.when(b == pl.num_programs(0) - 1)
    def _():
        for i in range(n):
            dkv_out[i][0] = (dk[i] * scale).astype(dkv_out[i].dtype)
            dkv_out[i][1] = dv[i].astype(dkv_out[i].dtype)


def combine_kernel(sc, own, above, below, *outs):
    for m in range(4):
        col = sc[0] ^ m
        for i in range(2):
            total = own[i, col] + above[i, col].astype(F32) + below[i, col].astype(F32)
            outs[m][i] = total.astype(outs[m].dtype)


def finish_kernel(sc, *refs):
    dq_in, dkv_in, (dq, dk, dv) = refs[:4], refs[4:8], refs[8:]
    for m in range(4):
        cols = lanes(sc[0] ^ m)
        dq[:, cols] = dq_in[m][...].astype(F32)
        dk[:, cols] = dkv_in[m][0].astype(F32)
        dv[:, cols] = dkv_in[m][1].astype(F32)


def assemble_kernel(sc, *refs):
    for m in range(4):
        refs[4][:, lanes(sc[0] ^ m)] = refs[m][...]


def outcome_kernel(sc, att, w_own, w_a, w_b, out):
    total = dot(att[:, lanes(sc[1])], w_own[:128], NN) + dot(att[:, lanes(sc[2])], w_own[128:], NN)
    total += dot(att[:, lanes(sc[3])], w_a[...], NN) + dot(att[:, lanes(sc[4])], w_b[...], NN)
    out[...] = total.astype(BF)


def weight_kernel(sc, att, att_other, g, g_other, own, other):
    width = own.shape[0]
    for ref, start in ((own, sc[1]), (other, sc[3])):
        cols = lanes(start, width)
        total = dot(att[:, cols], g[...], TN) + dot(att_other[:, cols], g_other[...], TN)
        ref[...] = total.astype(ref.dtype)


def place_rows_kernel(sc, *refs):
    size = refs[0].shape[0]
    for m in range(len(refs) - 1):
        refs[-1][pl.ds(pl.multiple_of((sc[0] ^ m) * size, size), size), :] = refs[m][...]


def place_final_kernel(sc, *refs):
    rows, cols = refs[0].shape
    for i in range(2):
        for j in range(2):
            at = pl.ds(pl.multiple_of((sc[0] ^ i) * rows, rows), rows)
            lane = pl.ds(pl.multiple_of((sc[1] ^ j) * cols, cols), cols)
            refs[4][at, lane] = refs[2 * i + j][...].astype(F32)


def ints(*values):
    return jnp.stack([jnp.asarray(v, jnp.int32) for v in values])


def on_device(query_in, key_in, value_in, grad_out, out_weight):
    clips, tile_rows, tile_cols, tile, feats = query_in.shape
    model = grad_out.shape[-1]
    head = feats // HEADS
    scale = head**-0.5
    assert (clips, tile_rows, tile_cols) == (1, 1, 1) and lax.axis_size("wa") == HEADS
    dp_size, ha_size = lax.axis_size("dp"), lax.axis_size("ha")
    fast = dp_size == 2 and ha_size == 4
    d, h, w = lax.axis_index("dp"), lax.axis_index("ha"), lax.axis_index("wa")
    core, yy = w & 1, w >> 1
    q2, k2, v2 = (a.reshape(tile, feats) for a in (query_in, key_in, value_in))
    g2 = grad_out.reshape(tile, model)
    half = model // 2

    if fast:
        mine = lax.dynamic_slice_in_dim(out_weight, core * head, head, 0)
        w_a = xor_send(mine, "dp", 1)
        w_b = xor_send(w_a, "wa", 1)
        w_own = out_weight
        first = 2 * (1 - d)
        heads_at = (2 * d, 2 * d + 1, first + core, first + 1 - core)
    else:
        whole = lax.all_gather(out_weight, "dp", axis=0, tiled=True)
        w_own, w_a, w_b = whole[: 2 * head], whole[2 * head : 3 * head], whole[3 * head :]
        heads_at = (0, 1, 2, 3)
    head_sc = ints(w, *heads_at)
    w_sc = ints(w)

    packed = call(
        pack_kernel, w_sc, [q2, k2, v2], [sds((2, tile, head), BF)] * 4 + [sds((tile, head), BF)] * 4
    )
    kv = [packed[0]] + [xor_send(packed[m], "wa", m) for m in (1, 2, 3)]
    qs = [packed[4]] + [xor_send(packed[4 + m], "wa", m) for m in (1, 2, 3)]
    above = [step_send(a, "ha", 1) for a in kv]
    below = [step_send(a, "ha", -1) for a in kv]

    steps = 4
    chunk = model // steps
    dos = call(
        grad_attn_kernel,
        head_sc,
        [g2, w_own, w_a, w_b],
        [sds((tile, head), BF)] * 4,
        grid=(steps,),
        in_specs=[pl.BlockSpec((a.shape[0], chunk), lambda i, _: (0, i)) for a in (g2, w_own, w_a, w_b)],
        scratch=[pltpu.VMEM((tile, feats), F32), pltpu.VMEM((4, tile, head), BF)],
        flops=2 * tile * model * feats,
    )
    dos = [dos[0]] + [xor_send(dos[m], "wa", m) for m in (1, 2, 3)]

    row_sc = ints(w, jnp.where(h > 0, 0, 1), jnp.where(h < ha_size - 1, 3, 2))
    pair = 2 * 30 * tile * tile * head
    by_tile = lambda shape: pl.BlockSpec((1,) + shape, lambda b, _: (b,) + (0,) * len(shape))
    outs = call(
        lambda *a: forward_kernel(scale * math.log2(math.e), *a),
        row_sc,
        qs + above + kv + below,
        [sds((tile, head), BF)] * 4
        + [sds((4, tile, head), BF), sds((4, tile, head), F32), sds((4, 3, 3, tile, tile), BF)],
        grid=(4,),
        out_specs=[None] * 4 + [by_tile((tile, head)), by_tile((tile, head)), by_tile((3, 3, tile, tile))],
        scratch=[
            pltpu.VMEM((3, 4, tile, head), BF),
            pltpu.VMEM((3, 4, tile, 2 * head), BF),
            pltpu.VMEM((4, tile, head), BF),
            pltpu.VMEM((9, tile, tile), F32),
            pltpu.VMEM((tile, 128), F32),
            pltpu.VMEM((tile, 2 * head), F32),
        ],
        flops=2 * pair,
        exps=30 * tile * tile,
    )
    att_m, (att_b, inv_b, probs) = outs[:4], outs[4:]
    att_m = [att_m[0]] + [xor_send(att_m[m], "wa", m) for m in (1, 2, 3)]

    def back(rows, extra):
        n = len(rows)
        halos = (above, kv, below)
        own = rows == (1,)
        args = qs + [a for r in rows for a in halos[r]] + dos + [att_b, inv_b] + [probs] * n + extra
        spec = lambda r: pl.BlockSpec((1, 1, 3, tile, tile), lambda b, _: (b, r, 0, 0, 0))
        in_specs = [None] * (8 + 4 * n) + [by_tile((tile, head))] * 2 + [spec(r) for r in rows]
        in_specs += [by_tile((tile, head))] * len(extra)
        if own:
            outs = [sds((tile, head), F32)] + [sds((tile, head), BF)] * 3 + [sds((2, 4, tile, head), F32)]
            out_specs = [None] * 5
        else:
            outs = [sds((4, tile, head), F32)] + [sds((2, 4, tile, head), BF)] * n
            out_specs = [by_tile((tile, head))] + [None] * n
        return call(
            lambda *a: backward_kernel(rows, scale, *a),
            row_sc,
            args,
            outs,
            grid=(4,),
            in_specs=in_specs,
            out_specs=out_specs,
            scratch=[pltpu.VMEM((n, 4, tile, head), BF)] * 2
            + [pltpu.VMEM((4, tile, head), BF)] * 2
            + [pltpu.VMEM((n, 4, tile, head), F32)] * 2
            + [pltpu.VMEM((tile, head), F32)],
            flops=4 * pair * n // 3,
        )

    dq_part, dkv_up, dkv_down = back((0, 2), [])
    from_below = step_send(dkv_up, "ha", -1)
    from_above = step_send(dkv_down, "ha", 1)
    *dq_m, dkv_own = back((1,), [dq_part])
    dq_m = [dq_m[0]] + [xor_send(dq_m[m], "wa", m) for m in (1, 2, 3)]
    dkv_m = call(
        combine_kernel,
        w_sc,
        [dkv_own, from_above, from_below],
        [sds((2, tile, head), F32)] + [sds((2, tile, head), BF)] * 3,
    )
    dkv_m = [dkv_m[0]] + [xor_send(dkv_m[m], "wa", m) for m in (1, 2, 3)]
    query_grad, key_grad, value_grad = call(
        finish_kernel, w_sc, dq_m + dkv_m, [sds((tile, feats), F32)] * 3
    )

    (att,) = call(assemble_kernel, w_sc, att_m, [sds((tile, feats), BF)])
    col = lambda a, n: pl.BlockSpec((a.shape[0], n), lambda i, _: (0, i))
    (outcome,) = call(
        outcome_kernel,
        head_sc,
        [att, w_own, w_a, w_b],
        [sds((tile, model), BF)],
        grid=(steps,),
        in_specs=[None] + [col(a, chunk) for a in (w_own, w_a, w_b)],
        out_specs=[pl.BlockSpec((tile, chunk), lambda i, _: (0, i))],
        flops=2 * tile * model * feats,
    )
    if fast:
        g_mine = lax.dynamic_slice_in_dim(g2, core * half, half, 1)
        g_other = xor_send(lax.dynamic_slice_in_dim(g2, (1 - core) * half, half, 1), "wa", 1)
        att_other = xor_send(att, "wa", 1)
        share = feats // 2
        wide = half // 2
        own, other = call(
            weight_kernel,
            ints(w, d, 0, 1 - d),
            [att, att_other, g_mine, g_other],
            [sds((share, half), F32), sds((share, half), BF)],
            grid=(2,),
            in_specs=[None, None, col(g_mine, wide), col(g_other, wide)],
            out_specs=[pl.BlockSpec((share, wide), lambda i, _: (0, i))] * 2,
            flops=4 * tile * feats * half,
        )
        total = own + xor_send(other, "dp", 1).astype(F32)
        rows = share // 2
        keep = lax.dynamic_slice_in_dim(total, yy * rows, rows, 0)
        send = lax.dynamic_slice_in_dim(total, (1 - yy) * rows, rows, 0).astype(BF)
        total = keep + xor_send(send, "wa", 2).astype(F32)
        rows = rows // 4
        keep = lax.dynamic_slice_in_dim(total, h * rows, rows, 0)
        for m in (1, 2, 3):
            send = lax.dynamic_slice_in_dim(total, (h ^ m) * rows, rows, 0).astype(BF)
            keep = keep + xor_send(send, "ha", m).astype(F32)
        piece = keep.astype(BF)
        pieces = [piece] + [xor_send(piece, "ha", m) for m in (1, 2, 3)]
        (piece,) = call(place_rows_kernel, ints(h), pieces, [sds((4 * rows, half), BF)])
        across = xor_send(piece, "wa", 2)
        pieces = [piece, xor_send(piece, "wa", 1), across, xor_send(across, "wa", 1)]
        (weight_grad,) = call(place_final_kernel, ints(yy, core), pieces, [sds((share, model), F32)])
    else:
        local = dot(att, g2, TN)
        summed = lax.psum(local, ("dp", "ha", "wa"))
        weight_grad = lax.dynamic_slice_in_dim(summed, d * (feats // dp_size), feats // dp_size, 0)
    return (
        outcome.reshape(grad_out.shape),
        query_grad.reshape(query_in.shape),
        key_grad.reshape(query_in.shape),
        value_grad.reshape(query_in.shape),
        weight_grad,
    )


def solution(mesh):
    tiles = P("dp", "ha", "wa", None, None)
    return jax.shard_map(
        on_device,
        mesh=mesh,
        in_specs=(tiles, tiles, tiles, tiles, P("dp", None)),
        out_specs=(tiles, tiles, tiles, tiles, P("dp", None)),
        check_vma=False,
    )
```

```python
import math

import jax
import jax.numpy as jnp
from jax import lax
from jax.experimental import pallas as pl
from jax.experimental.pallas import tpu as pltpu
from jax.sharding import PartitionSpec as P


HEADS = 4
BF = jnp.bfloat16
F32 = jnp.float32


def xor_send(value, axis, mask):
    count = lax.axis_size(axis)
    return lax.ppermute(value, axis, [(i, i ^ mask) for i in range(count)])


def step_send(value, axis, step):
    count = lax.axis_size(axis)
    pairs = [(i, i + step) for i in range(count) if 0 <= i + step < count]
    return lax.ppermute(value, axis, pairs)


def sds(shape, dtype):
    return jax.ShapeDtypeStruct(shape, dtype)


def full_spec(shape):
    zeros = (0,) * len(shape)
    return pl.BlockSpec(tuple(shape), lambda *_: zeros)


def place_of():
    d, h, w = lax.axis_index("dp"), lax.axis_index("ha"), lax.axis_index("wa")
    core, yy = w & 1, w >> 1
    heads_at = (0, 1, 2, 3)
    if lax.axis_size("dp") == 2:
        heads_at = (2 * d, 2 * d + 1, 2 - 2 * d, 3 - 2 * d)
    row_lo = jnp.where(h > 0, 0, 1)
    row_hi = jnp.where(h < lax.axis_size("ha") - 1, 3, 2)
    return (w, *heads_at, row_lo, row_hi, d, yy, h, core)


def call(kernel, args, outs, grid=(1,), in_specs=None, out_specs=None, scratch=(), flops=0, exps=0, alias=None):
    in_specs = [full_spec(a.shape) if s is None else s for a, s in zip(args, in_specs or [None] * len(args))]
    out_specs = [full_spec(o.shape) if s is None else s for o, s in zip(outs, out_specs or [None] * len(outs))]
    moved = sum(a.size * a.dtype.itemsize for a in args) + sum(o.size * jnp.dtype(o.dtype).itemsize for o in outs)
    return pl.pallas_call(
        lambda *refs: kernel(place_of(), *refs),
        out_shape=list(outs),
        grid=grid,
        in_specs=in_specs,
        out_specs=out_specs,
        scratch_shapes=list(scratch),
        input_output_aliases=alias or {},
        cost_estimate=pl.CostEstimate(flops=flops, transcendentals=exps, bytes_accessed=moved),
        compiler_params=pltpu.CompilerParams(
            dimension_semantics=("arbitrary",) * len(grid), vmem_limit_bytes=56 << 20
        ),
    )(*args)


def dot(a, b, dims):
    return lax.dot_general(a, b, (dims, ((), ())), preferred_element_type=F32)


NN = ((1,), (0,))
NT = ((1,), (1,))
TN = ((0,), (0,))


def lanes(index, width=128):
    return pl.ds(pl.multiple_of(index * width, width), width)


def pack_kernel(sc, q, k, v, *outs):
    w = sc[0]
    for far in range(2):
        for j in range(2):
            cols = lanes(w ^ (2 * far + j))
            outs[far][j, 0] = k[:, cols]
            outs[far][j, 1] = v[:, cols]
            outs[2 + far][j] = q[:, cols]


def stack_rows(core, own, even, odd, whole):
    size = own.shape[0]
    whole[:size, :] = own[...]

    @pl.when(core == 0)
    def _():
        whole[size:, :] = even[...]

    @pl.when(core == 1)
    def _():
        whole[size:, :] = odd[...]

    return whole[...]


def grad_attn_kernel(sc, g, w_own, w_even, w_odd, near, far, acc, by_head, whole):
    step = pl.program_id(0)
    part = dot(g[...], stack_rows(sc[10], w_own, w_even, w_odd, whole), NT)

    @pl.when(step == 0)
    def _():
        acc[...] = part

    @pl.when(step > 0)
    def _():
        acc[...] += part

    @pl.when(step == pl.num_programs(0) - 1)
    def _():
        for slot in range(4):
            by_head[sc[1 + slot]] = acc[:, slot * 128 : slot * 128 + 128].astype(BF)
        for j in range(2):
            near[j] = by_head[sc[0] ^ j]
            far[j] = by_head[sc[0] ^ (2 + j)]


def tile_rows_at(index, tile):
    return pl.ds(pl.multiple_of(index * tile, tile), tile)


def forward_kernel(factor, sc, *refs):
    q_in, kv_in = refs[:4], refs[4:16]
    near, far, att_b, inv_b, p_b = refs[16:21]
    ks, vs, qs, ss, mx, acc = refs[21:]
    tile = mx.shape[0]
    w, row_lo, row_hi = sc[0], sc[5], sc[6]
    step = pl.program_id(0)

    @pl.when(step == 0)
    def _():
        for m in range(4):
            at = tile_rows_at(w ^ m, tile)
            qs[at, :] = q_in[m][0]
            for r in range(3):
                ks[r, at, :] = kv_in[r * 4 + m][0, 0]
                vs[r, at, :128] = kv_in[r * 4 + m][0, 1]
                vs[r, at, 128:] = jnp.ones((tile, 128), BF)

    def one_tile(b):
        start, stop = max(b - 1, 0) * tile, min(b + 2, 4) * tile
        width = stop - start
        q = qs[b * tile : b * tile + tile, :]
        mx[...] = jnp.full(mx.shape, -jnp.inf, F32)

        def score_row(r, carry):
            s = dot(q, ks[r, start:stop, :], NT)
            ss[r, :, :width] = s
            best = mx[...]
            for i in range(width // 128):
                best = jnp.maximum(best, s[:, i * 128 : i * 128 + 128])
            mx[...] = best
            return carry

        lax.fori_loop(row_lo, row_hi, score_row, 0)
        top = jnp.max(mx[...], axis=1, keepdims=True)
        acc[...] = jnp.zeros_like(acc)

        def prob_row(r, carry):
            p = jnp.exp2((ss[r, :, :width] - top) * factor).astype(BF)
            p_b[0, r, :, :width] = p
            acc[...] += dot(p, vs[r, start:stop, :], NN)
            return carry

        lax.fori_loop(row_lo, row_hi, prob_row, 0)

    for b in range(4):
        pl.when(step == b)(lambda b=b: one_tile(b))
    inverse = 1.0 / acc[:, 128:]
    out = (acc[:, :128] * inverse).astype(BF)
    att_b[0] = out
    inv_b[0] = inverse
    for m in range(4):

        @pl.when((step ^ w) == m)
        def _():
            (near, far)[m // 2][m % 2] = out


def backward_kernel(row, scale, sc, *refs):
    q_in, kv_in, do_in = refs[:4], refs[4:8], refs[8:12]
    att_b, inv_b, p_in = refs[12:15]
    rest = refs[15:]
    dq_prev = None
    if row != 0:
        dq_prev, rest = rest[0], rest[1:]
    if row == 1:
        dq_near, dq_far, dkv_out, rest = rest[0], rest[1], rest[2], rest[3:]
    else:
        dq_out, dkv_out, rest = rest[0], rest[1], rest[2:]
    ks, vs, qs, dos, dk, dv, dq = rest
    tile = dq.shape[0]
    step = pl.program_id(0)
    w, row_lo, row_hi = sc[0], sc[5], sc[6]

    @pl.when(step == 0)
    def _():
        for m in range(4):
            at = tile_rows_at(w ^ m, tile)
            qs[at, :] = q_in[m][0]
            dos[at, :] = do_in[m][0]
            ks[at, :] = kv_in[m][0, 0]
            vs[at, :] = kv_in[m][0, 1]
        dk[...] = jnp.zeros_like(dk)
        dv[...] = jnp.zeros_like(dv)

    dq[...] = jnp.zeros_like(dq) if dq_prev is None else dq_prev[0]
    inverse = inv_b[0]
    here = tile_rows_at(step, tile)
    grad = dos[here, :].astype(F32)
    delta = jnp.sum(att_b[0].astype(F32) * grad, axis=1, keepdims=True) * inverse[:, :1]
    grad = (grad * inverse).astype(BF)
    q = qs[here, :]

    def one_tile(b):
        start, stop = max(b - 1, 0) * tile, min(b + 2, 4) * tile
        p = p_in[0, 0, :, : stop - start]
        dp = dot(grad, vs[start:stop, :], NT)
        ds = (p.astype(F32) * (dp - delta)).astype(BF)
        dq[...] += dot(ds, ks[start:stop, :], NN)
        dk[:, start:stop] += dot(q, ds, TN)
        dv[:, start:stop] += dot(grad, p, TN)

    valid = (row_lo <= row) & (row < row_hi)
    for b in range(4):
        pl.when((step == b) & valid)(lambda b=b: one_tile(b))

    if row != 1:
        dq_out[0] = dq[...]
    else:
        total = (dq[...] * scale).astype(BF)
        for m in range(4):

            @pl.when((step ^ w) == m)
            def _():
                (dq_near, dq_far)[m // 2][m % 2] = total

    @pl.when(step == pl.num_programs(0) - 1)
    def _():
        dkv_out[0] = (dk[...] * scale).T.astype(dkv_out.dtype)
        dkv_out[1] = dv[...].T.astype(dkv_out.dtype)


def combine_kernel(sc, own, above, below, near, far):
    tile = near.shape[2]
    for m in range(4):
        at = tile_rows_at(sc[0] ^ m, tile)
        for i in range(2):
            total = own[i, at, :] + above[i, at, :].astype(F32) + below[i, at, :].astype(F32)
            (near, far)[m // 2][m % 2, i] = total.astype(BF)


def finish_kernel(sc, *refs):
    dq_in, dkv_in, (dq, dk, dv) = refs[:4], refs[4:8], refs[8:]
    for m in range(4):
        cols = lanes(sc[0] ^ m)
        dq[:, cols] = dq_in[m][0].astype(F32)
        dk[:, cols] = dkv_in[m][0, 0].astype(F32)
        dv[:, cols] = dkv_in[m][0, 1].astype(F32)


def outcome_kernel(sc, near, p_near, far, p_far, w_own, w_even, w_odd, out, att, slots, whole):
    @pl.when(pl.program_id(0) == 0)
    def _():
        for m, piece in enumerate((near, p_near, far, p_far)):
            att[sc[0] ^ m] = piece[0]
        for slot in range(4):
            slots[:, slot * 128 : slot * 128 + 128] = att[sc[1 + slot]]

    out[...] = dot(slots[...], stack_rows(sc[10], w_own, w_even, w_odd, whole), NN).astype(BF)


def weight_kernel(sc, near, far, p_near, p_far, g, g_other, a_own, a_send, b_keep, b_send, att, slots, both, res):
    tile = g.shape[0]
    step = pl.program_id(0)
    w, d, yy = sc[0], sc[7], sc[8]

    @pl.when(step == 0)
    def _():
        for t in range(2):
            at = slice(t * tile, t * tile + tile)
            att[w, at, :] = near[t]
            att[w ^ 2, at, :] = far[t]
            att[w ^ 1, at, :] = p_near[1 - t]
            att[w ^ 3, at, :] = p_far[1 - t]
        for slot in range(4):
            slots[slot * 128 : slot * 128 + 128, :] = att[2 * (d ^ (slot // 2)) + slot % 2].T

    both[:tile, :] = g[...]
    both[tile:, :] = g_other[...]
    total = dot(slots[...], both[...], NN)

    @pl.when(step == 0)
    def _():
        a_own[...] = total[:256, :]
        a_send[...] = total[256:, :].astype(BF)

    @pl.when(step == 1)
    def _():
        res[...] = total
        for i in range(2):
            at = slice(i * 128, i * 128 + 128)
            b_keep[at, :] = res[lanes(2 * i + yy), :]
            b_send[at, :] = res[lanes(2 * i + 1 - yy), :].astype(BF)


def reduce_first_kernel(sc, a_own, a_in, b_keep, b_in, a_keep, a_send, b_own, b_send):
    yy = sc[8]
    mine, theirs = lanes(yy), lanes(1 - yy)
    a_keep[...] = a_own[mine, :] + a_in[mine, :].astype(F32)
    a_send[...] = (a_own[theirs, :] + a_in[theirs, :].astype(F32)).astype(BF)
    b_own[...] = b_keep[:128, :] + b_in[:128, :].astype(F32)
    b_send[...] = (b_keep[128:, :] + b_in[128:, :].astype(F32)).astype(BF)


def reduce_second_kernel(sc, a_keep, a_in, b_own, b_in, keep, *sends):
    rows, wide = keep.shape[0], a_keep.shape[1]
    for m in range(4):
        at = pl.ds(pl.multiple_of((sc[9] ^ m) * rows, rows), rows)
        left = a_keep[at, :] + a_in[at, :].astype(F32)
        right = b_own[at, :] + b_in[at, :].astype(F32)
        target = keep if m == 0 else sends[m - 1]
        target[:, :wide] = left.astype(target.dtype)
        target[:, wide:] = right.astype(target.dtype)


def place_rows_kernel(sc, *refs):
    size = refs[0].shape[0]
    for m in range(len(refs) - 1):
        refs[-1][pl.ds(pl.multiple_of((sc[9] ^ m) * size, size), size), :] = refs[m][...]


def place_final_kernel(sc, *refs):
    @pl.when(pl.program_id(0) == sc[10])
    def _():
        refs[-1][...] = refs[-3][...].astype(F32)

    @pl.when(pl.program_id(0) != sc[10])
    def _():
        refs[-1][...] = refs[-2][...].astype(F32)


def on_device(query_in, key_in, value_in, grad_out, out_weight):
    clips, tile_rows, tile_cols, tile, feats = query_in.shape
    model = grad_out.shape[-1]
    head = feats // HEADS
    scale = head**-0.5
    assert (clips, tile_rows, tile_cols) == (1, 1, 1) and lax.axis_size("wa") == HEADS
    dp_size, ha_size = lax.axis_size("dp"), lax.axis_size("ha")
    fast = dp_size == 2 and ha_size == 4
    d, w = lax.axis_index("dp"), lax.axis_index("wa")
    core = w & 1
    q2, k2, v2 = (a.reshape(tile, feats) for a in (query_in, key_in, value_in))
    g2 = grad_out.reshape(tile, model)
    half = model // 2

    def across(value):
        return xor_send(value, "wa", 2)

    def partner(value):
        return xor_send(value, "wa", 1)

    if fast:
        w_own = out_weight
        swap = [(HEADS * i + j, HEADS * (1 - i) + j) for i in range(2) for j in range(0, HEADS, 2)]
        w_even = lax.ppermute(out_weight, ("dp", "wa"), swap)
        w_odd = lax.ppermute(w_even, "wa", [(j, j + 1) for j in range(0, HEADS, 2)])
    else:
        whole = lax.all_gather(out_weight, "dp", axis=0, tiled=True)
        w_own, w_even = whole[: 2 * head], whole[2 * head :]
        w_odd = w_even

    kv_near, kv_far, q_near, q_far = call(
        pack_kernel, [q2, k2, v2], [sds((2, 2, tile, head), BF)] * 2 + [sds((2, tile, head), BF)] * 2
    )

    def gather(near, far):
        return [near, partner(near), far, partner(far)]

    kv_far = across(kv_far)
    q_far = across(q_far)
    kv = gather(kv_near, kv_far)
    qs = gather(q_near, q_far)
    above = gather(step_send(kv_near, "ha", 1), step_send(kv_far, "ha", 1))
    below = gather(step_send(kv_near, "ha", -1), step_send(kv_far, "ha", -1))

    def piece_specs(pieces):
        return [
            pl.BlockSpec((1,) + a.shape[1:], lambda *_, i=i, n=a.ndim: (i % 2,) + (0,) * (n - 1))
            for i, a in enumerate(pieces)
        ]

    steps = 4
    chunk = model // steps
    do_near, do_far = call(
        grad_attn_kernel,
        [g2, w_own, w_even, w_odd],
        [sds((2, tile, head), BF)] * 2,
        grid=(steps,),
        in_specs=[pl.BlockSpec((a.shape[0], chunk), lambda i: (0, i)) for a in (g2, w_own, w_even, w_odd)],
        scratch=[pltpu.VMEM((tile, feats), F32), pltpu.VMEM((4, tile, head), BF), pltpu.VMEM((feats, chunk), BF)],
        flops=2 * tile * model * feats,
    )
    dos = gather(do_near, across(do_far))

    pair = 2 * 30 * tile * tile * head

    def by_tile(*shape):
        return pl.BlockSpec((1,) + shape, lambda b: (b,) + (0,) * len(shape))

    halo = above + kv + below
    att_near, att_far, att_b, inv_b, probs = call(
        lambda *a: forward_kernel(scale * math.log2(math.e), *a),
        qs + halo,
        [sds((2, tile, head), BF)] * 2
        + [sds((4, tile, head), BF), sds((4, tile, head), F32), sds((4, 3, tile, 3 * tile), BF)],
        grid=(4,),
        in_specs=piece_specs(qs + halo),
        out_specs=[None] * 2 + [by_tile(tile, head), by_tile(tile, head), by_tile(3, tile, 3 * tile)],
        scratch=[
            pltpu.VMEM((3, 4 * tile, head), BF),
            pltpu.VMEM((3, 4 * tile, 2 * head), BF),
            pltpu.VMEM((4 * tile, head), BF),
            pltpu.VMEM((3, tile, 3 * tile), F32),
            pltpu.VMEM((tile, 128), F32),
            pltpu.VMEM((tile, 2 * head), F32),
        ],
        flops=2 * pair,
        exps=30 * tile * tile,
    )
    atts = gather(att_near, across(att_far))
    near, p_near, far, p_far = atts

    def back(row, extra):
        pieces = qs + (above, kv, below)[row] + dos
        p_spec = pl.BlockSpec((1, 1, tile, 3 * tile), lambda b: (b, row, 0, 0))
        if row == 1:
            outs = [sds((2, tile, head), BF)] * 2 + [sds((2, 4 * tile, head), F32)]
            out_specs = [None] * 3
        else:
            outs = [sds((4, tile, head), F32), sds((2, 4 * tile, head), BF)]
            out_specs = [by_tile(tile, head), None]
        return call(
            lambda *a: backward_kernel(row, scale, *a),
                pieces + [att_b, inv_b, probs] + extra,
            outs,
            grid=(4,),
            in_specs=piece_specs(pieces) + [by_tile(tile, head)] * 2 + [p_spec] + [by_tile(tile, head)] * len(extra),
            out_specs=out_specs,
            scratch=[pltpu.VMEM((4 * tile, head), BF)] * 4
            + [pltpu.VMEM((head, 4 * tile), F32)] * 2
            + [pltpu.VMEM((tile, head), F32)],
            flops=4 * pair // 3,
        )

    dq_part, dkv_up = back(0, [])
    dq_part, dkv_down = back(2, [dq_part])
    dq_near, dq_far, dkv_own = back(1, [dq_part])
    from_below = step_send(dkv_up, "ha", -1)
    from_above = step_send(dkv_down, "ha", 1)
    dqs = gather(dq_near, across(dq_far))
    dkv_near, dkv_far = call(combine_kernel, [dkv_own, from_above, from_below], [sds((2, 2, tile, head), BF)] * 2)
    dkvs = gather(dkv_near, across(dkv_far))
    query_grad, key_grad, value_grad = call(
        finish_kernel, dqs + dkvs, [sds((tile, feats), F32)] * 3,
        in_specs=piece_specs(dqs + dkvs),
    )

    def cols(a, n):
        return pl.BlockSpec((a.shape[0], n), lambda i: (0, i))

    (outcome,) = call(
        outcome_kernel,
        atts + [w_own, w_even, w_odd],
        [sds((tile, model), BF)],
        grid=(steps,),
        in_specs=piece_specs(atts) + [cols(a, chunk) for a in (w_own, w_even, w_odd)],
        out_specs=[pl.BlockSpec((tile, chunk), lambda i: (0, i))],
        scratch=[pltpu.VMEM((4, tile, head), BF), pltpu.VMEM((tile, feats), BF), pltpu.VMEM((feats, chunk), BF)],
        flops=2 * tile * model * feats,
    )
    if fast:
        g_mine = lax.dynamic_slice_in_dim(g2, core * half, half, 1)
        g_other = partner(lax.dynamic_slice_in_dim(g2, (1 - core) * half, half, 1))
        share, wide = feats // 2, half // 2
        a_own, a_send, b_keep, b_send = call(
            weight_kernel,
                [near, far, p_near, p_far, g_mine, g_other],
            [sds((share, wide), F32), sds((share, wide), BF)] * 2,
            grid=(2,),
            in_specs=[None] * 4 + [cols(g_mine, wide), cols(g_other, wide)],
            scratch=[
                pltpu.VMEM((4, 2 * tile, head), BF),
                pltpu.VMEM((feats, 2 * tile), BF),
                pltpu.VMEM((2 * tile, wide), BF),
                pltpu.VMEM((feats, wide), F32),
            ],
            flops=4 * tile * feats * half,
        )
        a_in = xor_send(a_send, "dp", 1)
        b_in = across(b_send)
        a_own, a_send, b_keep, b_send = call(
            reduce_first_kernel,
                [a_own, a_in, b_keep, b_in],
            [sds((share // 2, wide), F32), sds((share // 2, wide), BF)] * 2,
        )
        a_in = across(a_send)
        b_in = xor_send(b_send, "dp", 1)
        rows = share // 8
        keep, *sends = call(
            reduce_second_kernel, [a_own, a_in, b_keep, b_in], [sds((rows, half), F32)] + [sds((rows, half), BF)] * 3
        )
        got = [xor_send(sends[m - 1], "ha", m) for m in (1, 2, 3)]
        piece = (keep + got[0].astype(F32) + got[1].astype(F32) + got[2].astype(F32)).astype(BF)
        pieces = [piece] + [xor_send(piece, "ha", m) for m in (1, 2, 3)]
        (piece,) = call(place_rows_kernel, pieces, [sds((4 * rows, half), BF)])
        other = across(piece)

        def rows_of(flip):
            return pl.BlockSpec((share // 2, half), lambda j: ((lax.axis_index("wa") >> 1) ^ flip, j))

        (begun,) = call(
            place_final_kernel, [piece, partner(piece)], [sds((share, model), F32)], grid=(2,), out_specs=[rows_of(0)]
        )
        (weight_grad,) = call(
            place_final_kernel,
            [begun, other, partner(other)],
            [sds((share, model), F32)],
            grid=(2,),
            in_specs=[pl.BlockSpec(memory_space=pl.ANY), None, None],
            out_specs=[rows_of(1)],
            alias={0: 0},
        )
    else:
        att = jnp.zeros((tile, feats), BF)
        for m, value in enumerate((near[0], p_near[1], far[0], p_far[1])):
            att = lax.dynamic_update_slice_in_dim(att, value, (w ^ m) * head, 1)
        local = dot(att, g2, TN)
        summed = lax.psum(local, ("dp", "ha", "wa"))
        weight_grad = lax.dynamic_slice_in_dim(summed, d * (feats // dp_size), feats // dp_size, 0)
    return (
        outcome.reshape(grad_out.shape),
        query_grad.reshape(query_in.shape),
        key_grad.reshape(query_in.shape),
        value_grad.reshape(query_in.shape),
        weight_grad,
    )


def solution(mesh):
    tiles = P("dp", "ha", "wa", None, None)
    return jax.shard_map(
        on_device,
        mesh=mesh,
        in_specs=(tiles, tiles, tiles, tiles, P("dp", None)),
        out_specs=(tiles, tiles, tiles, tiles, P("dp", None)),
        check_vma=False,
    )
```

```python
import math

import jax
import jax.numpy as jnp
from jax import lax
from jax.experimental import pallas as pl
from jax.experimental.pallas import tpu as pltpu
from jax.sharding import PartitionSpec as P


HEADS = 4
BF = jnp.bfloat16
F32 = jnp.float32


def xor_send(value, axis, mask):
    count = lax.axis_size(axis)
    return lax.ppermute(value, axis, [(i, i ^ mask) for i in range(count)])


def step_send(value, axis, step):
    count = lax.axis_size(axis)
    pairs = [(i, i + step) for i in range(count) if 0 <= i + step < count]
    return lax.ppermute(value, axis, pairs)


def sds(shape, dtype):
    return jax.ShapeDtypeStruct(shape, dtype)


def full_spec(shape):
    zeros = (0,) * len(shape)
    return pl.BlockSpec(tuple(shape), lambda *_: zeros)


def place_of():
    d, h, w = lax.axis_index("dp"), lax.axis_index("ha"), lax.axis_index("wa")
    core, yy = w & 1, w >> 1
    heads_at = (0, 1, 2, 3)
    if lax.axis_size("dp") == 2:
        heads_at = (2 * d, 2 * d + 1, 2 - 2 * d, 3 - 2 * d)
    row_lo = jnp.where(h > 0, 0, 1)
    row_hi = jnp.where(h < lax.axis_size("ha") - 1, 3, 2)
    return (w, *heads_at, row_lo, row_hi, d, yy, h, core)


def call(kernel, args, outs, grid=(1,), in_specs=None, out_specs=None, scratch=(), flops=0, exps=0, alias=None):
    in_specs = [full_spec(a.shape) if s is None else s for a, s in zip(args, in_specs or [None] * len(args))]
    out_specs = [full_spec(o.shape) if s is None else s for o, s in zip(outs, out_specs or [None] * len(outs))]
    moved = sum(a.size * a.dtype.itemsize for a in args) + sum(o.size * jnp.dtype(o.dtype).itemsize for o in outs)
    return pl.pallas_call(
        lambda *refs: kernel(place_of(), *refs),
        out_shape=list(outs),
        grid=grid,
        in_specs=in_specs,
        out_specs=out_specs,
        scratch_shapes=list(scratch),
        input_output_aliases=alias or {},
        cost_estimate=pl.CostEstimate(flops=flops, transcendentals=exps, bytes_accessed=moved),
        compiler_params=pltpu.CompilerParams(
            dimension_semantics=("arbitrary",) * len(grid), vmem_limit_bytes=56 << 20
        ),
    )(*args)


def dot(a, b, dims):
    return lax.dot_general(a, b, (dims, ((), ())), preferred_element_type=F32)


NN = ((1,), (0,))
NT = ((1,), (1,))
TN = ((0,), (0,))


def lanes(index, width=128):
    return pl.ds(pl.multiple_of(index * width, width), width)


def pack_kernel(sc, q, k, v, *outs):
    w = sc[0]
    for far in range(2):
        for j in range(2):
            cols = lanes(w ^ (2 * far + j))
            outs[far][j, 0] = k[:, cols]
            outs[far][j, 1] = v[:, cols]
            outs[2 + far][j] = q[:, cols]


def grad_attn_kernel(sc, g, w_own, w_even, w_odd, near, far, acc, by_head):
    step = pl.program_id(0)

    @pl.when(step == 0)
    def _():
        acc[...] = jnp.zeros_like(acc)

    acc[:, :256] += dot(g[...], w_own[...], NT)
    for core, rows in enumerate((w_even, w_odd)):

        @pl.when(sc[10] == core)
        def _():
            acc[:, 256:] += dot(g[...], rows[...], NT)

    @pl.when(step == pl.num_programs(0) - 1)
    def _():
        for slot in range(4):
            by_head[sc[1 + slot]] = acc[:, slot * 128 : slot * 128 + 128].astype(BF)
        for j in range(2):
            near[j] = by_head[sc[0] ^ j]
            far[j] = by_head[sc[0] ^ (2 + j)]


def tile_rows_at(index, tile):
    return pl.ds(pl.multiple_of(index * tile, tile), tile)


def forward_kernel(factor, sc, *refs):
    q_in, kv_in = refs[:4], refs[4:16]
    near, far, att_b, inv_b, p_b = refs[16:21]
    ks, vs, qs, ss, mx, acc = refs[21:]
    tile = mx.shape[0]
    w, row_lo, row_hi = sc[0], sc[5], sc[6]
    step = pl.program_id(0)

    @pl.when(step == 0)
    def _():
        for m in range(4):
            at = tile_rows_at(w ^ m, tile)
            qs[at, :] = q_in[m][0]
            for r in range(3):
                ks[r, at, :] = kv_in[r * 4 + m][0, 0]
                vs[r, at, :128] = kv_in[r * 4 + m][0, 1]
                vs[r, at, 128:] = jnp.ones((tile, 128), BF)

    def one_tile(b):
        start, stop = max(b - 1, 0) * tile, min(b + 2, 4) * tile
        width = stop - start
        q = qs[b * tile : b * tile + tile, :]
        mx[...] = jnp.full(mx.shape, -jnp.inf, F32)

        def score_row(r, carry):
            s = dot(q, ks[r, start:stop, :], NT)
            ss[r, :, :width] = s
            best = mx[...]
            for i in range(width // 128):
                best = jnp.maximum(best, s[:, i * 128 : i * 128 + 128])
            mx[...] = best
            return carry

        lax.fori_loop(row_lo, row_hi, score_row, 0)
        top = jnp.max(mx[...], axis=1, keepdims=True)
        acc[...] = jnp.zeros_like(acc)

        def prob_row(r, carry):
            p = jnp.exp2((ss[r, :, :width] - top) * factor).astype(BF)
            p_b[0, r, :, :width] = p
            acc[...] += dot(p, vs[r, start:stop, :], NN)
            return carry

        lax.fori_loop(row_lo, row_hi, prob_row, 0)

    for b in range(4):
        pl.when(step == b)(lambda b=b: one_tile(b))
    inverse = 1.0 / acc[:, 128:]
    out = (acc[:, :128] * inverse).astype(BF)
    att_b[0] = out
    inv_b[0] = inverse
    for m in range(4):

        @pl.when((step ^ w) == m)
        def _():
            (near, far)[m // 2][m % 2] = out


def backward_kernel(row, scale, sc, *refs):
    q_in, kv_in, do_in = refs[:4], refs[4:8], refs[8:12]
    att_b, inv_b, p_in = refs[12:15]
    rest = refs[15:]
    dq_prev = None
    if row != 0:
        dq_prev, rest = rest[0], rest[1:]
    if row == 1:
        dq_near, dq_far, dkv_out, rest = rest[0], rest[1], rest[2], rest[3:]
    else:
        dq_out, dkv_out, rest = rest[0], rest[1], rest[2:]
    ks, vs, qs, dos, dk, dv, dq = rest
    tile = dq.shape[0]
    step = pl.program_id(0)
    w, row_lo, row_hi = sc[0], sc[5], sc[6]

    @pl.when(step == 0)
    def _():
        for m in range(4):
            at = tile_rows_at(w ^ m, tile)
            qs[at, :] = q_in[m][0]
            dos[at, :] = do_in[m][0]
            ks[at, :] = kv_in[m][0, 0]
            vs[at, :] = kv_in[m][0, 1]
        dk[...] = jnp.zeros_like(dk)
        dv[...] = jnp.zeros_like(dv)

    dq[...] = jnp.zeros_like(dq) if dq_prev is None else dq_prev[0]
    inverse = inv_b[0]
    here = tile_rows_at(step, tile)
    grad = dos[here, :].astype(F32)
    delta = jnp.sum(att_b[0].astype(F32) * grad, axis=1, keepdims=True) * inverse[:, :1]
    grad = (grad * inverse).astype(BF)
    q = qs[here, :]

    def one_tile(b):
        start, stop = max(b - 1, 0) * tile, min(b + 2, 4) * tile
        p = p_in[0, 0, :, : stop - start]
        dp = dot(grad, vs[start:stop, :], NT)
        ds = (p.astype(F32) * (dp - delta)).astype(BF)
        dq[...] += dot(ds, ks[start:stop, :], NN)
        dk[:, start:stop] += dot(q, ds, TN)
        dv[:, start:stop] += dot(grad, p, TN)

    valid = (row_lo <= row) & (row < row_hi)
    for b in range(4):
        pl.when((step == b) & valid)(lambda b=b: one_tile(b))

    if row != 1:
        dq_out[0] = dq[...]
    else:
        total = (dq[...] * scale).astype(BF)
        for m in range(4):

            @pl.when((step ^ w) == m)
            def _():
                (dq_near, dq_far)[m // 2][m % 2] = total

    @pl.when(step == pl.num_programs(0) - 1)
    def _():
        dkv_out[0] = (dk[...] * scale).T.astype(dkv_out.dtype)
        dkv_out[1] = dv[...].T.astype(dkv_out.dtype)


def combine_kernel(sc, own, above, below, near, far):
    tile = near.shape[2]
    for m in range(4):
        at = tile_rows_at(sc[0] ^ m, tile)
        for i in range(2):
            total = own[i, at, :] + above[i, at, :].astype(F32) + below[i, at, :].astype(F32)
            (near, far)[m // 2][m % 2, i] = total.astype(BF)


def finish_kernel(sc, *refs):
    dq_in, dkv_in, (dq, dk, dv) = refs[:4], refs[4:8], refs[8:]
    for m in range(4):
        cols = lanes(sc[0] ^ m)
        dq[:, cols] = dq_in[m][0].astype(F32)
        dk[:, cols] = dkv_in[m][0, 0].astype(F32)
        dv[:, cols] = dkv_in[m][0, 1].astype(F32)


def outcome_kernel(sc, near, p_near, far, p_far, w_own, w_even, w_odd, out, att, slots):
    @pl.when(pl.program_id(0) == 0)
    def _():
        for m, piece in enumerate((near, p_near, far, p_far)):
            att[sc[0] ^ m] = piece[0]
        for slot in range(4):
            slots[:, slot * 128 : slot * 128 + 128] = att[sc[1 + slot]]

    for core, rows in enumerate((w_even, w_odd)):

        @pl.when(sc[10] == core)
        def _():
            total = dot(slots[:, :256], w_own[...], NN) + dot(slots[:, 256:], rows[...], NN)
            out[...] = total.astype(BF)


def weight_kernel(sc, near, far, p_near, p_far, g, g_other, a_own, a_send, b_keep, b_send, att, slots, both, res):
    tile = g.shape[0]
    step = pl.program_id(0)
    w, d, yy = sc[0], sc[7], sc[8]

    @pl.when(step == 0)
    def _():
        for t in range(2):
            at = slice(t * tile, t * tile + tile)
            att[w, at, :] = near[t]
            att[w ^ 2, at, :] = far[t]
            att[w ^ 1, at, :] = p_near[1 - t]
            att[w ^ 3, at, :] = p_far[1 - t]
        for slot in range(4):
            slots[slot * 128 : slot * 128 + 128, :] = att[2 * (d ^ (slot // 2)) + slot % 2].T

    both[:tile, :] = g[...]
    both[tile:, :] = g_other[...]
    total = dot(slots[...], both[...], NN)

    @pl.when(step == 0)
    def _():
        a_own[...] = total[:256, :]
        a_send[...] = total[256:, :].astype(BF)

    @pl.when(step == 1)
    def _():
        res[...] = total
        for i in range(2):
            at = slice(i * 128, i * 128 + 128)
            b_keep[at, :] = res[lanes(2 * i + yy), :]
            b_send[at, :] = res[lanes(2 * i + 1 - yy), :].astype(BF)


def reduce_first_kernel(sc, a_own, a_in, b_keep, b_in, a_keep, a_send, b_own, b_send):
    yy = sc[8]
    mine, theirs = lanes(yy), lanes(1 - yy)
    a_keep[...] = a_own[mine, :] + a_in[mine, :].astype(F32)
    a_send[...] = (a_own[theirs, :] + a_in[theirs, :].astype(F32)).astype(BF)
    b_own[...] = b_keep[:128, :] + b_in[:128, :].astype(F32)
    b_send[...] = (b_keep[128:, :] + b_in[128:, :].astype(F32)).astype(BF)


def reduce_second_kernel(sc, a_keep, a_in, b_own, b_in, keep, *sends):
    rows, wide = keep.shape[0], a_keep.shape[1]
    for m in range(4):
        at = pl.ds(pl.multiple_of((sc[9] ^ m) * rows, rows), rows)
        left = a_keep[at, :] + a_in[at, :].astype(F32)
        right = b_own[at, :] + b_in[at, :].astype(F32)
        target = keep if m == 0 else sends[m - 1]
        target[:, :wide] = left.astype(target.dtype)
        target[:, wide:] = right.astype(target.dtype)


def place_rows_kernel(sc, *refs):
    size = refs[0].shape[0]
    for m in range(len(refs) - 1):
        refs[-1][pl.ds(pl.multiple_of((sc[9] ^ m) * size, size), size), :] = refs[m][...]


def place_final_kernel(sc, *refs):
    @pl.when(pl.program_id(0) == sc[10])
    def _():
        refs[-1][...] = refs[-3][...].astype(F32)

    @pl.when(pl.program_id(0) != sc[10])
    def _():
        refs[-1][...] = refs[-2][...].astype(F32)


def on_device(query_in, key_in, value_in, grad_out, out_weight):
    clips, tile_rows, tile_cols, tile, feats = query_in.shape
    model = grad_out.shape[-1]
    head = feats // HEADS
    scale = head**-0.5
    assert (clips, tile_rows, tile_cols) == (1, 1, 1) and lax.axis_size("wa") == HEADS
    dp_size, ha_size = lax.axis_size("dp"), lax.axis_size("ha")
    fast = dp_size == 2 and ha_size == 4
    d, w = lax.axis_index("dp"), lax.axis_index("wa")
    core = w & 1
    q2, k2, v2 = (a.reshape(tile, feats) for a in (query_in, key_in, value_in))
    g2 = grad_out.reshape(tile, model)
    half = model // 2

    def across(value):
        return xor_send(value, "wa", 2)

    def partner(value):
        return xor_send(value, "wa", 1)

    if fast:
        w_own = out_weight
        swap = [(HEADS * i + j, HEADS * (1 - i) + j) for i in range(2) for j in range(0, HEADS, 2)]
        w_even = lax.ppermute(out_weight, ("dp", "wa"), swap)
        w_odd = lax.ppermute(w_even, "wa", [(j, j + 1) for j in range(0, HEADS, 2)])
    else:
        whole = lax.all_gather(out_weight, "dp", axis=0, tiled=True)
        w_own, w_even = whole[: 2 * head], whole[2 * head :]
        w_odd = w_even

    kv_near, kv_far, q_near, q_far = call(
        pack_kernel,
        [q2, k2, v2],
        [sds((2, 2, tile, head), BF)] * 2 + [sds((2, tile, head), BF)] * 2,
    )

    def gather(near, far):
        return [near, partner(near), far, partner(far)]

    kv_far = across(kv_far)
    q_far = across(q_far)
    kv = gather(kv_near, kv_far)
    qs = gather(q_near, q_far)
    above = gather(step_send(kv_near, "ha", 1), step_send(kv_far, "ha", 1))
    below = gather(step_send(kv_near, "ha", -1), step_send(kv_far, "ha", -1))

    def piece_specs(pieces):
        return [
            pl.BlockSpec((1,) + a.shape[1:], lambda *_, i=i, n=a.ndim: (i % 2,) + (0,) * (n - 1))
            for i, a in enumerate(pieces)
        ]

    steps = 4
    chunk = model // steps
    do_near, do_far = call(
        grad_attn_kernel,
        [g2, w_own, w_even, w_odd],
        [sds((2, tile, head), BF)] * 2,
        grid=(steps,),
        in_specs=[pl.BlockSpec((a.shape[0], chunk), lambda i: (0, i)) for a in (g2, w_own, w_even, w_odd)],
        scratch=[pltpu.VMEM((tile, feats), F32), pltpu.VMEM((4, tile, head), BF)],
        flops=2 * tile * model * feats,
    )
    dos = gather(do_near, across(do_far))

    pair = 2 * 30 * tile * tile * head

    def by_tile(*shape):
        return pl.BlockSpec((1,) + shape, lambda b: (b,) + (0,) * len(shape))

    halo = above + kv + below
    att_near, att_far, att_b, inv_b, probs = call(
        lambda *a: forward_kernel(scale * math.log2(math.e), *a),
        qs + halo,
        [sds((2, tile, head), BF)] * 2
        + [sds((4, tile, head), BF), sds((4, tile, head), F32), sds((4, 3, tile, 3 * tile), BF)],
        grid=(4,),
        in_specs=piece_specs(qs + halo),
        out_specs=[None] * 2 + [by_tile(tile, head), by_tile(tile, head), by_tile(3, tile, 3 * tile)],
        scratch=[
            pltpu.VMEM((3, 4 * tile, head), BF),
            pltpu.VMEM((3, 4 * tile, 2 * head), BF),
            pltpu.VMEM((4 * tile, head), BF),
            pltpu.VMEM((3, tile, 3 * tile), F32),
            pltpu.VMEM((tile, 128), F32),
            pltpu.VMEM((tile, 2 * head), F32),
        ],
        flops=2 * pair,
        exps=30 * tile * tile,
    )
    atts = gather(att_near, across(att_far))
    near, p_near, far, p_far = atts

    def back(row, extra):
        pieces = qs + (above, kv, below)[row] + dos
        p_spec = pl.BlockSpec((1, 1, tile, 3 * tile), lambda b: (b, row, 0, 0))
        if row == 1:
            outs = [sds((2, tile, head), BF)] * 2 + [sds((2, 4 * tile, head), F32)]
            out_specs = [None] * 3
        else:
            outs = [sds((4, tile, head), F32), sds((2, 4 * tile, head), BF)]
            out_specs = [by_tile(tile, head), None]
        return call(
            lambda *a: backward_kernel(row, scale, *a),
                pieces + [att_b, inv_b, probs] + extra,
            outs,
            grid=(4,),
            in_specs=piece_specs(pieces) + [by_tile(tile, head)] * 2 + [p_spec] + [by_tile(tile, head)] * len(extra),
            out_specs=out_specs,
            scratch=[pltpu.VMEM((4 * tile, head), BF)] * 4
            + [pltpu.VMEM((head, 4 * tile), F32)] * 2
            + [pltpu.VMEM((tile, head), F32)],
            flops=4 * pair // 3,
        )

    dq_part, dkv_up = back(0, [])
    dq_part, dkv_down = back(2, [dq_part])
    dq_near, dq_far, dkv_own = back(1, [dq_part])
    from_below = step_send(dkv_up, "ha", -1)
    from_above = step_send(dkv_down, "ha", 1)
    dqs = gather(dq_near, across(dq_far))
    dkv_near, dkv_far = call(
        combine_kernel, [dkv_own, from_above, from_below], [sds((2, 2, tile, head), BF)] * 2
    )
    dkvs = gather(dkv_near, across(dkv_far))
    query_grad, key_grad, value_grad = call(
        finish_kernel, dqs + dkvs, [sds((tile, feats), F32)] * 3,
        in_specs=piece_specs(dqs + dkvs),
    )

    def cols(a, n):
        return pl.BlockSpec((a.shape[0], n), lambda i: (0, i))

    (outcome,) = call(
        outcome_kernel,
        atts + [w_own, w_even, w_odd],
        [sds((tile, model), BF)],
        grid=(steps,),
        in_specs=piece_specs(atts) + [cols(a, chunk) for a in (w_own, w_even, w_odd)],
        out_specs=[pl.BlockSpec((tile, chunk), lambda i: (0, i))],
        scratch=[pltpu.VMEM((4, tile, head), BF), pltpu.VMEM((tile, feats), BF)],
        flops=2 * tile * model * feats,
    )
    if fast:
        g_mine = lax.dynamic_slice_in_dim(g2, core * half, half, 1)
        g_other = partner(lax.dynamic_slice_in_dim(g2, (1 - core) * half, half, 1))
        share, wide = feats // 2, half // 2
        a_own, a_send, b_keep, b_send = call(
            weight_kernel,
                [near, far, p_near, p_far, g_mine, g_other],
            [sds((share, wide), F32), sds((share, wide), BF)] * 2,
            grid=(2,),
            in_specs=[None] * 4 + [cols(g_mine, wide), cols(g_other, wide)],
            scratch=[
                pltpu.VMEM((4, 2 * tile, head), BF),
                pltpu.VMEM((feats, 2 * tile), BF),
                pltpu.VMEM((2 * tile, wide), BF),
                pltpu.VMEM((feats, wide), F32),
            ],
            flops=4 * tile * feats * half,
        )
        a_in = xor_send(a_send, "dp", 1)
        b_in = across(b_send)
        a_own, a_send, b_keep, b_send = call(
            reduce_first_kernel,
                [a_own, a_in, b_keep, b_in],
            [sds((share // 2, wide), F32), sds((share // 2, wide), BF)] * 2,
            grid=(2,),
            in_specs=[cols(a_own, wide // 2)] * 4,
            out_specs=[pl.BlockSpec((share // 2, wide // 2), lambda i: (0, i))] * 4,
        )
        a_in = across(a_send)
        b_in = xor_send(b_send, "dp", 1)
        rows = share // 8
        keep, *sends = call(
            reduce_second_kernel,
                [a_own, a_in, b_keep, b_in],
            [sds((rows, half), F32)] + [sds((rows, half), BF)] * 3,
        )
        got = [xor_send(sends[m - 1], "ha", m) for m in (1, 2, 3)]
        piece = (keep + got[0].astype(F32) + got[1].astype(F32) + got[2].astype(F32)).astype(BF)
        pieces = [piece] + [xor_send(piece, "ha", m) for m in (1, 2, 3)]
        (piece,) = call(place_rows_kernel, pieces, [sds((4 * rows, half), BF)])
        other = across(piece)

        def rows_of(flip):
            return pl.BlockSpec((share // 2, half), lambda j: ((lax.axis_index("wa") >> 1) ^ flip, j))

        (begun,) = call(
            place_final_kernel,
            [piece, partner(piece)],
            [sds((share, model), F32)],
            grid=(2,),
            out_specs=[rows_of(0)],
        )
        (weight_grad,) = call(
            place_final_kernel,
            [begun, other, partner(other)],
            [sds((share, model), F32)],
            grid=(2,),
            in_specs=[pl.BlockSpec(memory_space=pl.ANY), None, None],
            out_specs=[rows_of(1)],
            alias={0: 0},
        )
    else:
        att = jnp.zeros((tile, feats), BF)
        for m, value in enumerate((near[0], p_near[1], far[0], p_far[1])):
            att = lax.dynamic_update_slice_in_dim(att, value, (w ^ m) * head, 1)
        local = dot(att, g2, TN)
        summed = lax.psum(local, ("dp", "ha", "wa"))
        weight_grad = lax.dynamic_slice_in_dim(summed, d * (feats // dp_size), feats // dp_size, 0)
    return (
        outcome.reshape(grad_out.shape),
        query_grad.reshape(query_in.shape),
        key_grad.reshape(query_in.shape),
        value_grad.reshape(query_in.shape),
        weight_grad,
    )


def solution(mesh):
    tiles = P("dp", "ha", "wa", None, None)
    return jax.shard_map(
        on_device,
        mesh=mesh,
        in_specs=(tiles, tiles, tiles, tiles, P("dp", None)),
        out_specs=(tiles, tiles, tiles, tiles, P("dp", None)),
        check_vma=False,
    )
```

```python
import math

import jax
import jax.numpy as jnp
from jax import lax
from jax.experimental import pallas as pl
from jax.experimental.pallas import tpu as pltpu
from jax.sharding import PartitionSpec as P


HEADS = 4
BF = jnp.bfloat16
F32 = jnp.float32


def xor_send(value, axis, mask):
    count = lax.axis_size(axis)
    return lax.ppermute(value, axis, [(i, i ^ mask) for i in range(count)])


def step_send(value, axis, step):
    count = lax.axis_size(axis)
    pairs = [(i, i + step) for i in range(count) if 0 <= i + step < count]
    return lax.ppermute(value, axis, pairs)


def sds(shape, dtype):
    return jax.ShapeDtypeStruct(shape, dtype)


def full_spec(shape):
    zeros = (0,) * len(shape)
    return pl.BlockSpec(tuple(shape), lambda *_: zeros)


def place_of():
    d, h, w = lax.axis_index("dp"), lax.axis_index("ha"), lax.axis_index("wa")
    core, yy = w & 1, w >> 1
    heads_at = (0, 1, 2, 3)
    if lax.axis_size("dp") == 2:
        heads_at = (2 * d, 2 * d + 1, 2 - 2 * d, 3 - 2 * d)
    row_lo = jnp.where(h > 0, 0, 1)
    row_hi = jnp.where(h < lax.axis_size("ha") - 1, 3, 2)
    return (w, *heads_at, row_lo, row_hi, d, yy, h, core)


def call(kernel, args, outs, grid=(1,), in_specs=None, out_specs=None, scratch=(), flops=0, exps=0, alias=None):
    in_specs = [full_spec(a.shape) if s is None else s for a, s in zip(args, in_specs or [None] * len(args))]
    out_specs = [full_spec(o.shape) if s is None else s for o, s in zip(outs, out_specs or [None] * len(outs))]
    moved = sum(a.size * a.dtype.itemsize for a in args) + sum(o.size * jnp.dtype(o.dtype).itemsize for o in outs)
    return pl.pallas_call(
        lambda *refs: kernel(place_of(), *refs),
        out_shape=list(outs),
        grid=grid,
        in_specs=in_specs,
        out_specs=out_specs,
        scratch_shapes=list(scratch),
        input_output_aliases=alias or {},
        cost_estimate=pl.CostEstimate(flops=flops, transcendentals=exps, bytes_accessed=moved),
        compiler_params=pltpu.CompilerParams(
            dimension_semantics=("arbitrary",) * len(grid), vmem_limit_bytes=56 << 20
        ),
    )(*args)


def dot(a, b, dims):
    return lax.dot_general(a, b, (dims, ((), ())), preferred_element_type=F32)


NN = ((1,), (0,))
NT = ((1,), (1,))
TN = ((0,), (0,))


def lanes(index, width=128):
    return pl.ds(pl.multiple_of(index * width, width), width)


def pack_kernel(sc, q, k, v, *outs):
    w = sc[0]
    for far in range(2):
        for j in range(2):
            cols = lanes(w ^ (2 * far + j))
            outs[far][j, 0] = k[:, cols]
            outs[far][j, 1] = v[:, cols]
            outs[2 + far][j] = q[:, cols]


def grad_attn_kernel(sc, g, w_own, w_even, w_odd, near, far, acc, by_head):
    step = pl.program_id(0)

    @pl.when(step == 0)
    def _():
        acc[...] = jnp.zeros_like(acc)

    acc[:, :256] += dot(g[...], w_own[...], NT)
    for core, rows in enumerate((w_even, w_odd)):

        @pl.when(sc[10] == core)
        def _():
            acc[:, 256:] += dot(g[...], rows[...], NT)

    @pl.when(step == pl.num_programs(0) - 1)
    def _():
        for slot in range(4):
            by_head[sc[1 + slot]] = acc[:, slot * 128 : slot * 128 + 128].astype(BF)
        for j in range(2):
            near[j] = by_head[sc[0] ^ j]
            far[j] = by_head[sc[0] ^ (2 + j)]


def tile_rows_at(index, tile):
    return pl.ds(pl.multiple_of(index * tile, tile), tile)


def forward_kernel(factor, sc, *refs):
    q_in, kv_in = refs[:4], refs[4:16]
    near, far, att_b, inv_b, p_b = refs[16:21]
    ks, vs, qs, ss, mx, acc = refs[21:]
    tile = mx.shape[0]
    w, row_lo, row_hi = sc[0], sc[5], sc[6]
    step = pl.program_id(0)

    @pl.when(step == 0)
    def _():
        for m in range(4):
            at = tile_rows_at(w ^ m, tile)
            qs[at, :] = q_in[m][0]
            for r in range(3):
                ks[r, at, :] = kv_in[r * 4 + m][0, 0]
                vs[r, at, :128] = kv_in[r * 4 + m][0, 1]
                vs[r, at, 128:] = jnp.ones((tile, 128), BF)

    def one_tile(b):
        start, stop = max(b - 1, 0) * tile, min(b + 2, 4) * tile
        width = stop - start
        q = qs[b * tile : b * tile + tile, :]
        mx[...] = jnp.full(mx.shape, -jnp.inf, F32)

        def score_row(r, carry):
            s = dot(q, ks[r, start:stop, :], NT)
            ss[r, :, :width] = s
            best = mx[...]
            for i in range(width // 128):
                best = jnp.maximum(best, s[:, i * 128 : i * 128 + 128])
            mx[...] = best
            return carry

        lax.fori_loop(row_lo, row_hi, score_row, 0)
        top = jnp.max(mx[...], axis=1, keepdims=True)
        acc[...] = jnp.zeros_like(acc)

        def prob_row(r, carry):
            p = jnp.exp2((ss[r, :, :width] - top) * factor).astype(BF)
            p_b[0, r, :, :width] = p
            acc[...] += dot(p, vs[r, start:stop, :], NN)
            return carry

        lax.fori_loop(row_lo, row_hi, prob_row, 0)

    for b in range(4):
        pl.when(step == b)(lambda b=b: one_tile(b))
    inverse = 1.0 / acc[:, 128:]
    out = (acc[:, :128] * inverse).astype(BF)
    att_b[0] = out
    inv_b[0] = inverse
    for m in range(4):

        @pl.when((step ^ w) == m)
        def _():
            (near, far)[m // 2][m % 2] = out


def backward_kernel(row, scale, sc, *refs):
    q_in, kv_in, do_in = refs[:4], refs[4:8], refs[8:12]
    att_b, inv_b, p_in = refs[12:15]
    rest = refs[15:]
    dq_prev = None
    if row != 0:
        dq_prev, rest = rest[0], rest[1:]
    if row == 1:
        dq_near, dq_far, dkv_out, rest = rest[0], rest[1], rest[2], rest[3:]
    else:
        dq_out, dkv_out, rest = rest[0], rest[1], rest[2:]
    ks, vs, qs, dos, dk, dv, dq = rest
    tile = dq.shape[0]
    step = pl.program_id(0)
    w, row_lo, row_hi = sc[0], sc[5], sc[6]

    @pl.when(step == 0)
    def _():
        for m in range(4):
            at = tile_rows_at(w ^ m, tile)
            qs[at, :] = q_in[m][0]
            dos[at, :] = do_in[m][0]
            ks[at, :] = kv_in[m][0, 0]
            vs[at, :] = kv_in[m][0, 1]
        dk[...] = jnp.zeros_like(dk)
        dv[...] = jnp.zeros_like(dv)

    dq[...] = jnp.zeros_like(dq) if dq_prev is None else dq_prev[0]
    inverse = inv_b[0]
    here = tile_rows_at(step, tile)
    grad = dos[here, :].astype(F32)
    delta = jnp.sum(att_b[0].astype(F32) * grad, axis=1, keepdims=True) * inverse[:, :1]
    grad = (grad * inverse).astype(BF)
    q = qs[here, :]

    def one_tile(b):
        start, stop = max(b - 1, 0) * tile, min(b + 2, 4) * tile
        p = p_in[0, 0, :, : stop - start]
        dp = dot(grad, vs[start:stop, :], NT)
        ds = (p.astype(F32) * (dp - delta)).astype(BF)
        dq[...] += dot(ds, ks[start:stop, :], NN)
        dk[:, start:stop] += dot(q, ds, TN)
        dv[:, start:stop] += dot(grad, p, TN)

    valid = (row_lo <= row) & (row < row_hi)
    for b in range(4):
        pl.when((step == b) & valid)(lambda b=b: one_tile(b))

    if row != 1:
        dq_out[0] = dq[...]
    else:
        total = (dq[...] * scale).astype(BF)
        for m in range(4):

            @pl.when((step ^ w) == m)
            def _():
                (dq_near, dq_far)[m // 2][m % 2] = total

    @pl.when(step == pl.num_programs(0) - 1)
    def _():
        dkv_out[0] = (dk[...] * scale).T.astype(dkv_out.dtype)
        dkv_out[1] = dv[...].T.astype(dkv_out.dtype)


def combine_kernel(sc, own, above, below, near, far):
    tile = near.shape[2]
    for m in range(4):
        at = tile_rows_at(sc[0] ^ m, tile)
        for i in range(2):
            total = own[i, at, :] + above[i, at, :].astype(F32) + below[i, at, :].astype(F32)
            (near, far)[m // 2][m % 2, i] = total.astype(BF)


def finish_kernel(sc, *refs):
    dq_in, dkv_in, (dq, dk, dv) = refs[:4], refs[4:8], refs[8:]
    for m in range(4):
        cols = lanes(sc[0] ^ m)
        dq[:, cols] = dq_in[m][0].astype(F32)
        dk[:, cols] = dkv_in[m][0, 0].astype(F32)
        dv[:, cols] = dkv_in[m][0, 1].astype(F32)


def outcome_kernel(sc, near, p_near, far, p_far, w_own, w_even, w_odd, out, att, slots):
    @pl.when(pl.program_id(0) == 0)
    def _():
        for m, piece in enumerate((near, p_near, far, p_far)):
            att[sc[0] ^ m] = piece[0]
        for slot in range(4):
            slots[:, slot * 128 : slot * 128 + 128] = att[sc[1 + slot]]

    for core, rows in enumerate((w_even, w_odd)):

        @pl.when(sc[10] == core)
        def _():
            total = dot(slots[:, :256], w_own[...], NN) + dot(slots[:, 256:], rows[...], NN)
            out[...] = total.astype(BF)


def weight_kernel(sc, near, far, p_near, p_far, g, g_other, a_own, a_send, b_keep, b_send, att, slots, both, res):
    tile = g.shape[0]
    step = pl.program_id(0)
    w, d, yy = sc[0], sc[7], sc[8]

    @pl.when(step == 0)
    def _():
        for t in range(2):
            at = slice(t * tile, t * tile + tile)
            att[w, at, :] = near[t]
            att[w ^ 2, at, :] = far[t]
            att[w ^ 1, at, :] = p_near[1 - t]
            att[w ^ 3, at, :] = p_far[1 - t]
        for slot in range(4):
            slots[slot * 128 : slot * 128 + 128, :] = att[2 * (d ^ (slot // 2)) + slot % 2].T

    both[:tile, :] = g[...]
    both[tile:, :] = g_other[...]
    total = dot(slots[...], both[...], NN)

    @pl.when(step == 0)
    def _():
        a_own[...] = total[:256, :]
        a_send[...] = total[256:, :].astype(BF)

    @pl.when(step == 1)
    def _():
        res[...] = total
        for i in range(2):
            at = slice(i * 128, i * 128 + 128)
            b_keep[at, :] = res[lanes(2 * i + yy), :]
            b_send[at, :] = res[lanes(2 * i + 1 - yy), :].astype(BF)


def reduce_first_kernel(sc, a_own, a_in, b_keep, b_in, a_keep, a_send, b_own, b_send):
    yy = sc[8]
    mine, theirs = lanes(yy), lanes(1 - yy)
    a_keep[...] = a_own[mine, :] + a_in[mine, :].astype(F32)
    a_send[...] = (a_own[theirs, :] + a_in[theirs, :].astype(F32)).astype(BF)
    b_own[...] = b_keep[:128, :] + b_in[:128, :].astype(F32)
    b_send[...] = (b_keep[128:, :] + b_in[128:, :].astype(F32)).astype(BF)


def reduce_second_kernel(sc, a_keep, a_in, b_own, b_in, keep, *sends):
    rows, wide = keep.shape[0], a_keep.shape[1]
    for m in range(4):
        at = pl.ds(pl.multiple_of((sc[9] ^ m) * rows, rows), rows)
        left = a_keep[at, :] + a_in[at, :].astype(F32)
        right = b_own[at, :] + b_in[at, :].astype(F32)
        target = keep if m == 0 else sends[m - 1]
        target[:, :wide] = left.astype(target.dtype)
        target[:, wide:] = right.astype(target.dtype)


def place_final_kernel(sc, *refs):
    out = refs[-1]
    size = refs[-2].shape[0]
    column = pl.program_id(0)
    for mine, pieces in ((True, refs[-9:-5]), (False, refs[-5:-1])):

        @pl.when((column == sc[10]) if mine else (column != sc[10]))
        def _():
            for m in range(4):
                at = pl.ds(pl.multiple_of((sc[9] ^ m) * size, size), size)
                out[at, :] = pieces[m][...].astype(F32)


def on_device(query_in, key_in, value_in, grad_out, out_weight):
    clips, tile_rows, tile_cols, tile, feats = query_in.shape
    model = grad_out.shape[-1]
    head = feats // HEADS
    scale = head**-0.5
    assert (clips, tile_rows, tile_cols) == (1, 1, 1) and lax.axis_size("wa") == HEADS
    dp_size, ha_size = lax.axis_size("dp"), lax.axis_size("ha")
    fast = dp_size == 2 and ha_size == 4
    d, w = lax.axis_index("dp"), lax.axis_index("wa")
    core = w & 1
    q2, k2, v2 = (a.reshape(tile, feats) for a in (query_in, key_in, value_in))
    g2 = grad_out.reshape(tile, model)
    half = model // 2

    def across(value):
        return xor_send(value, "wa", 2)

    def partner(value):
        return xor_send(value, "wa", 1)

    if fast:
        w_own = out_weight
        swap = [(HEADS * i + j, HEADS * (1 - i) + j) for i in range(2) for j in range(0, HEADS, 2)]
        w_even = lax.ppermute(out_weight, ("dp", "wa"), swap)
        w_odd = lax.ppermute(w_even, "wa", [(j, j + 1) for j in range(0, HEADS, 2)])
    else:
        whole = lax.all_gather(out_weight, "dp", axis=0, tiled=True)
        w_own, w_even = whole[: 2 * head], whole[2 * head :]
        w_odd = w_even

    kv_near, kv_far, q_near, q_far = call(
        pack_kernel,
        [q2, k2, v2],
        [sds((2, 2, tile, head), BF)] * 2 + [sds((2, tile, head), BF)] * 2,
    )

    def gather(near, far):
        return [near, partner(near), far, partner(far)]

    kv_far = across(kv_far)
    q_far = across(q_far)
    kv = gather(kv_near, kv_far)
    qs = gather(q_near, q_far)
    above = gather(step_send(kv_near, "ha", 1), step_send(kv_far, "ha", 1))
    below = gather(step_send(kv_near, "ha", -1), step_send(kv_far, "ha", -1))

    def piece_specs(pieces):
        return [
            pl.BlockSpec((1,) + a.shape[1:], lambda *_, i=i, n=a.ndim: (i % 2,) + (0,) * (n - 1))
            for i, a in enumerate(pieces)
        ]

    steps = 4
    chunk = model // steps
    do_near, do_far = call(
        grad_attn_kernel,
        [g2, w_own, w_even, w_odd],
        [sds((2, tile, head), BF)] * 2,
        grid=(steps,),
        in_specs=[pl.BlockSpec((a.shape[0], chunk), lambda i: (0, i)) for a in (g2, w_own, w_even, w_odd)],
        scratch=[pltpu.VMEM((tile, feats), F32), pltpu.VMEM((4, tile, head), BF)],
        flops=2 * tile * model * feats,
    )
    dos = gather(do_near, across(do_far))

    pair = 2 * 30 * tile * tile * head

    def by_tile(*shape):
        return pl.BlockSpec((1,) + shape, lambda b: (b,) + (0,) * len(shape))

    halo = above + kv + below
    att_near, att_far, att_b, inv_b, probs = call(
        lambda *a: forward_kernel(scale * math.log2(math.e), *a),
        qs + halo,
        [sds((2, tile, head), BF)] * 2
        + [sds((4, tile, head), BF), sds((4, tile, head), F32), sds((4, 3, tile, 3 * tile), BF)],
        grid=(4,),
        in_specs=piece_specs(qs + halo),
        out_specs=[None] * 2 + [by_tile(tile, head), by_tile(tile, head), by_tile(3, tile, 3 * tile)],
        scratch=[
            pltpu.VMEM((3, 4 * tile, head), BF),
            pltpu.VMEM((3, 4 * tile, 2 * head), BF),
            pltpu.VMEM((4 * tile, head), BF),
            pltpu.VMEM((3, tile, 3 * tile), F32),
            pltpu.VMEM((tile, 128), F32),
            pltpu.VMEM((tile, 2 * head), F32),
        ],
        flops=2 * pair,
        exps=30 * tile * tile,
    )
    atts = gather(att_near, across(att_far))
    near, p_near, far, p_far = atts

    def back(row, extra):
        pieces = qs + (above, kv, below)[row] + dos
        p_spec = pl.BlockSpec((1, 1, tile, 3 * tile), lambda b: (b, row, 0, 0))
        if row == 1:
            outs = [sds((2, tile, head), BF)] * 2 + [sds((2, 4 * tile, head), F32)]
            out_specs = [None] * 3
        else:
            outs = [sds((4, tile, head), F32), sds((2, 4 * tile, head), BF)]
            out_specs = [by_tile(tile, head), None]
        return call(
            lambda *a: backward_kernel(row, scale, *a),
                pieces + [att_b, inv_b, probs] + extra,
            outs,
            grid=(4,),
            in_specs=piece_specs(pieces) + [by_tile(tile, head)] * 2 + [p_spec] + [by_tile(tile, head)] * len(extra),
            out_specs=out_specs,
            scratch=[pltpu.VMEM((4 * tile, head), BF)] * 4
            + [pltpu.VMEM((head, 4 * tile), F32)] * 2
            + [pltpu.VMEM((tile, head), F32)],
            flops=4 * pair // 3,
        )

    dq_part, dkv_up = back(0, [])
    dq_part, dkv_down = back(2, [dq_part])
    dq_near, dq_far, dkv_own = back(1, [dq_part])
    from_below = step_send(dkv_up, "ha", -1)
    from_above = step_send(dkv_down, "ha", 1)
    dqs = gather(dq_near, across(dq_far))
    dkv_near, dkv_far = call(
        combine_kernel, [dkv_own, from_above, from_below], [sds((2, 2, tile, head), BF)] * 2
    )
    dkvs = gather(dkv_near, across(dkv_far))
    query_grad, key_grad, value_grad = call(
        finish_kernel, dqs + dkvs, [sds((tile, feats), F32)] * 3,
        in_specs=piece_specs(dqs + dkvs),
    )

    def cols(a, n):
        return pl.BlockSpec((a.shape[0], n), lambda i: (0, i))

    (outcome,) = call(
        outcome_kernel,
        atts + [w_own, w_even, w_odd],
        [sds((tile, model), BF)],
        grid=(steps,),
        in_specs=piece_specs(atts) + [cols(a, chunk) for a in (w_own, w_even, w_odd)],
        out_specs=[pl.BlockSpec((tile, chunk), lambda i: (0, i))],
        scratch=[pltpu.VMEM((4, tile, head), BF), pltpu.VMEM((tile, feats), BF)],
        flops=2 * tile * model * feats,
    )
    if fast:
        g_mine = lax.dynamic_slice_in_dim(g2, core * half, half, 1)
        g_other = partner(lax.dynamic_slice_in_dim(g2, (1 - core) * half, half, 1))
        share, wide = feats // 2, half // 2
        a_own, a_send, b_keep, b_send = call(
            weight_kernel,
                [near, far, p_near, p_far, g_mine, g_other],
            [sds((share, wide), F32), sds((share, wide), BF)] * 2,
            grid=(2,),
            in_specs=[None] * 4 + [cols(g_mine, wide), cols(g_other, wide)],
            scratch=[
                pltpu.VMEM((4, 2 * tile, head), BF),
                pltpu.VMEM((feats, 2 * tile), BF),
                pltpu.VMEM((2 * tile, wide), BF),
                pltpu.VMEM((feats, wide), F32),
            ],
            flops=4 * tile * feats * half,
        )
        a_in = xor_send(a_send, "dp", 1)
        b_in = across(b_send)
        a_own, a_send, b_keep, b_send = call(
            reduce_first_kernel,
                [a_own, a_in, b_keep, b_in],
            [sds((share // 2, wide), F32), sds((share // 2, wide), BF)] * 2,
            grid=(2,),
            in_specs=[cols(a_own, wide // 2)] * 4,
            out_specs=[pl.BlockSpec((share // 2, wide // 2), lambda i: (0, i))] * 4,
        )
        a_in = across(a_send)
        b_in = xor_send(b_send, "dp", 1)
        rows = share // 8
        keep, *sends = call(
            reduce_second_kernel,
                [a_own, a_in, b_keep, b_in],
            [sds((rows, half), F32)] + [sds((rows, half), BF)] * 3,
        )
        got = [xor_send(sends[m - 1], "ha", m) for m in (1, 2, 3)]
        piece = (keep + got[0].astype(F32) + got[1].astype(F32) + got[2].astype(F32)).astype(BF)
        pieces = [piece] + [xor_send(piece, "ha", m) for m in (1, 2, 3)]
        others = [across(value) for value in pieces]
        near_pieces = pieces + [partner(value) for value in pieces]
        far_pieces = others + [partner(value) for value in others]

        def rows_of(flip):
            return pl.BlockSpec((share // 2, half), lambda j: ((lax.axis_index("wa") >> 1) ^ flip, j))

        (begun,) = call(
            place_final_kernel,
            near_pieces,
            [sds((share, model), F32)],
            grid=(2,),
            out_specs=[rows_of(0)],
        )
        (weight_grad,) = call(
            place_final_kernel,
            [begun] + far_pieces,
            [sds((share, model), F32)],
            grid=(2,),
            in_specs=[pl.BlockSpec(memory_space=pl.ANY)] + [None] * 8,
            out_specs=[rows_of(1)],
            alias={0: 0},
        )
    else:
        att = jnp.zeros((tile, feats), BF)
        for m, value in enumerate((near[0], p_near[1], far[0], p_far[1])):
            att = lax.dynamic_update_slice_in_dim(att, value, (w ^ m) * head, 1)
        local = dot(att, g2, TN)
        summed = lax.psum(local, ("dp", "ha", "wa"))
        weight_grad = lax.dynamic_slice_in_dim(summed, d * (feats // dp_size), feats // dp_size, 0)
    return (
        outcome.reshape(grad_out.shape),
        query_grad.reshape(query_in.shape),
        key_grad.reshape(query_in.shape),
        value_grad.reshape(query_in.shape),
        weight_grad,
    )


def solution(mesh):
    tiles = P("dp", "ha", "wa", None, None)
    return jax.shard_map(
        on_device,
        mesh=mesh,
        in_specs=(tiles, tiles, tiles, tiles, P("dp", None)),
        out_specs=(tiles, tiles, tiles, tiles, P("dp", None)),
        check_vma=False,
    )
```
